128 devices in a mesh: row: 8 (over x_hi, z), col: 16 (over y, x_lo, core).
Axes of the slice: x: 4 (x_hi: 2, x_lo: 2; x = x_hi * 2 + x_lo), y: 4, z: 4, core: 2. Of those that a mesh axis runs over, the one named last changes fastest.
Arguments:
- coeffs: float32 [8192, 8192], P('row', 'col'), may hold values from -6 to 6
- hamiltonian_tiles: float32 [16, 4, 512, 512], P('col'), may hold values from -0.125 to 0.125
- source_lists: int32 [16, 3], P('col'), may hold values from 0 to 15, as said below
- present: int32 [16, 4, 4, 4], P('col'), may hold values 0 or 1
Outputs:
- sigma_vector: float32 [8192, 8192], P('row', 'col')
The draws below stay inside these ranges and needn't reach their ends.
Inputs may be any that keep to these rules, and one draw needn't show every extreme that they name: `source_lists`: each row names 3 different tiles, never its own; every tile is named by some row.
All inputs are finite; a program needn't handle non-finite values. No bound on the sum of `present` on one device may be relied on, other than what follows from the above.
Results may differ from the reference program's by a relative error of at most 0.0003.
Values sent between devices are 32-bit elements; how exact they have to be, the bound alone decides.
No kernel may reach another device: no remote copies, remote signals or barrier semaphores. Data moves between devices by JAX's collectives and lax.ppermute only.
A program may use at most 192 MiB of HBM per device.

```python
import jax
import jax.numpy as jnp
from jax import lax

TILE_STRINGS = 512
BLOCK_STRINGS = 128
SLOT_COUNT = 4
TILE_COUNT = 16
W = 8192


def draw_source_lists(key, part):
    first_key = jax.random.fold_in(key, 11)
    second_key = jax.random.fold_in(key, 23)
    cycle_order = jax.random.permutation(first_key, TILE_COUNT).astype(jnp.int32)
    following = jnp.roll(cycle_order, -1)
    first_listed = jnp.zeros((TILE_COUNT,), jnp.int32).at[cycle_order].set(following)
    positions = jnp.arange(TILE_COUNT, dtype=jnp.int32)
    scores = jax.random.randint(second_key, (TILE_COUNT, TILE_COUNT), 0, 1 << 20, dtype=jnp.int32) * TILE_COUNT + positions[None, :]
    banned = (positions[None, :] == positions[:, None]) | (positions[None, :] == first_listed[:, None])
    scores = jnp.where(banned, -1, scores)
    ranking = jnp.argsort(-scores, axis=1, stable=True).astype(jnp.int32)
    return jnp.stack([first_listed, ranking[:, 0], ranking[:, 1]], axis=1).astype(jnp.int32)


def with_ends(drawn, stream_key, low, largest):
    longest = drawn.shape.index(max(drawn.shape))
    spots = []
    for shift in (0, 1):
        where = [jax.random.randint(jax.random.fold_in(stream_key, axis), (), 0, length) for axis, length in enumerate(drawn.shape)]
        where[longest] = (where[longest] + shift) % drawn.shape[longest]
        spots.append(tuple(where))
    return drawn.at[spots[0]].set(low).at[spots[1]].set(largest)


def shard_levels(rng, dims, split, low, largest):
    factor_of = 1.0
    for axis_at, blocks in split:
        draws = jax.random.uniform(jax.random.fold_in(jax.random.fold_in(rng, 6), axis_at), (blocks,), jnp.float32, low / len(split), largest / len(split))
        factor_of = factor_of * jnp.repeat(jnp.exp(draws), dims[axis_at] // blocks).reshape((-1,) + (1,) * (len(dims) - 1 - axis_at))
    return factor_of


def centred(rng, dims, deviation, most, cuts=(), held_as=jnp.bfloat16):
    level = shard_levels(rng, dims, cuts, -0.22, 0.18) if cuts else 1.0
    entries = jax.random.normal(rng, dims, jnp.float32) * deviation * level
    return jnp.minimum(jnp.maximum(entries, -most), most).astype(held_as)


def setup_inputs(seed: int = 0) -> dict:
    keys = jax.random.split(jax.random.key(seed), 5)
    coeffs = centred(keys[0], (W, W), 1.0, 6.0, ((0, 8), (1, 16)), jnp.float32)
    hamiltonian_tiles = centred(keys[1], (TILE_COUNT, SLOT_COUNT, TILE_STRINGS, TILE_STRINGS), (SLOT_COUNT * TILE_STRINGS) ** -0.5, 0.125, ((0, 16),), jnp.float32)
    source_lists = draw_source_lists(jax.random.fold_in(keys[4], 71), 0)
    present = with_ends((jax.random.randint(keys[3], (TILE_COUNT, SLOT_COUNT, TILE_STRINGS // BLOCK_STRINGS, TILE_STRINGS // BLOCK_STRINGS), 0, 5) < 4).astype(jnp.int32), jax.random.fold_in(keys[3], 1), 0, 1)
    return dict(coeffs=coeffs, hamiltonian_tiles=hamiltonian_tiles, source_lists=source_lists, present=present)


def expand_mask(present_tile):
    return jnp.repeat(jnp.repeat(present_tile, BLOCK_STRINGS, axis=-2), BLOCK_STRINGS, axis=-1)


def product(left, right):
    return jnp.dot(left, right, precision=lax.Precision.HIGHEST, preferred_element_type=jnp.float32)


def reference(coeffs, hamiltonian_tiles, source_lists, present):
    masked = hamiltonian_tiles * expand_mask(present).astype(jnp.float32)

    def one_column(column):
        sources = jnp.concatenate([column[None].astype(jnp.int32), source_lists[column].astype(jnp.int32)])
        blocks = masked[column]
        total = jnp.zeros((W, TILE_STRINGS), jnp.float32)
        for index_of_slot in range(SLOT_COUNT):
            start_col = (sources[index_of_slot] * TILE_STRINGS).astype(jnp.int32)
            piece = lax.dynamic_slice_in_dim(coeffs, start_col, TILE_STRINGS, 1)
            total = total + product(piece, blocks[index_of_slot])
        return total

    column_list = lax.map(one_column, jnp.arange(TILE_COUNT, dtype=jnp.int32))
    halfsum = jnp.transpose(column_list, (1, 0, 2)).reshape(W, W)
    return halfsum + halfsum.T
```

```python
import jax
import jax.numpy as jnp
from jax import lax
from jax.experimental import pallas as pl
from jax.experimental.pallas import tpu as pltpu
from jax.sharding import Mesh, PartitionSpec as P

SIZES = (2, 4, 4, 2, 2)
AXES = ("xh", "z", "y", "xl", "core")
T = 512
HALF = 256
B = 128

SWAP = [(0, 1), (1, 0)]
OUTER = [(0, 3), (3, 0), (1, 2), (2, 1)]


def along_y(step):
    return [(i, (i + step) % 4) for i in range(4)]


def split(value):
    high = value.astype(jnp.bfloat16)
    return high, (value - high.astype(jnp.float32)).astype(jnp.bfloat16)


def dot(left, right):
    return jnp.dot(left, right, preferred_element_type=jnp.float32)


def half_kernel(table, mask, *refs):
    tiles, rest = refs[:16], refs[16:]
    own_m, core_m = rest[0], rest[1]
    far_m, rest = rest[2:10], rest[10:]
    mirror_out, near_out, far_out, c_all, c_high, c_low, m_all, c_sem, m_sem = rest
    for i in range(16):
        pltpu.make_async_copy(tiles[i], c_all.at[i], c_sem.at[i]).start()
    for i in range(4):
        pltpu.make_async_copy(own_m.at[i], m_all.at[i], m_sem.at[i]).start()
    for i in range(4):
        pltpu.make_async_copy(core_m.at[i], m_all.at[4 + i], m_sem.at[4 + i]).start()
    for i in range(8):
        pltpu.make_async_copy(far_m[i], m_all.at[8 + i], m_sem.at[8 + i]).start()
    for i in range(16):
        pltpu.make_async_copy(tiles[i], c_all.at[i], c_sem.at[i]).wait()

    def split_tile(i, carry):
        high, low = split(c_all[i])
        c_high[i] = high
        c_low[i] = low
        return carry

    lax.fori_loop(0, 16, split_tile, 0)
    xl, core = table[16], table[17]

    def column(j, carry):
        total = jnp.zeros((HALF, T), jnp.float32)
        for m in range(4):
            jm = j * 4 + m
            pltpu.make_async_copy(own_m.at[0], m_all.at[jm], m_sem.at[jm]).wait()
            t = table[jm]
            left_high, left_low = c_high[t], c_low[t]
            for bi in range(4):
                rows = slice(bi * B, (bi + 1) * B)
                flags = jnp.concatenate(
                    [
                        jnp.full((1, B), mask[jm * 16 + bi * 4 + bj].astype(jnp.float32), jnp.float32)
                        for bj in range(4)
                    ],
                    axis=1,
                )
                m_all[jm, rows, :] = m_all[jm, rows, :] * flags
            high, low = split(m_all[jm])
            total = total + (dot(left_high, high) + (dot(left_high, low) + dot(left_low, high)))
        dx, dc = j // 2, j % 2
        mirror_out[:, (xl + dx) % 2, (core + dc) % 2] = total.reshape(32, 8, T)

        @pl.when(dx == 0)
        def _():
            near_out[dc] = total

        @pl.when(dx == 1)
        def _():
            far_out[dc] = total

        return carry

    lax.fori_loop(0, 4, column, 0)


def half_products(table, mask, tiles, own_m, core_m, far_m):
    anywhere = pl.BlockSpec(memory_space=pl.ANY)
    vmem = pl.BlockSpec(memory_space=pltpu.VMEM)
    return pl.pallas_call(
        half_kernel,
        out_shape=(
            jax.ShapeDtypeStruct((32, 2, 2, 8, T), jnp.float32),
            jax.ShapeDtypeStruct((2, HALF, T), jnp.float32),
            jax.ShapeDtypeStruct((2, HALF, T), jnp.float32),
        ),
        grid_spec=pltpu.PrefetchScalarGridSpec(
            num_scalar_prefetch=2,
            grid=(),
            in_specs=[anywhere] * 26,
            out_specs=(vmem, vmem, vmem),
            scratch_shapes=[
                pltpu.VMEM((16, HALF, T), jnp.float32),
                pltpu.VMEM((16, HALF, T), jnp.bfloat16),
                pltpu.VMEM((16, HALF, T), jnp.bfloat16),
                pltpu.VMEM((16, T, T), jnp.float32),
                pltpu.SemaphoreType.DMA((16,)),
                pltpu.SemaphoreType.DMA((16,)),
            ],
        ),
        compiler_params=pltpu.CompilerParams(vmem_limit_bytes=44 << 20),
        cost_estimate=pl.CostEstimate(
            flops=3 * 2 * 16 * HALF * T * T, bytes_accessed=28 << 20, transcendentals=0
        ),
        name="half_products",
    )(table, mask, *tiles, own_m, core_m, *far_m)


def join_kernel(place, d00, d01, d10, d11, mirror, out):
    xl, core = place[0], place[1]
    for ds in range(2):
        for dh in range(2):
            slot = (core + ds) % 2
            half = (xl + dh) % 2
            direct = ((d00, d01), (d10, d11))[ds][dh]
            columns = pl.ds(pl.multiple_of(half * HALF, HALF), HALF)
            for h in range(2):
                turned = mirror[:, h, slot, :, columns].reshape(HALF, HALF).T
                piece = direct[:, h * HALF : (h + 1) * HALF] + turned
                out[pl.ds(pl.multiple_of((slot * 2 + half) * HALF, HALF), HALF), h * HALF : (h + 1) * HALF] = piece


def join(place, d00, d01, d10, d11, mirror):
    vmem = pl.BlockSpec(memory_space=pltpu.VMEM)
    return pl.pallas_call(
        join_kernel,
        out_shape=jax.ShapeDtypeStruct((2 * T, T), jnp.float32),
        grid_spec=pltpu.PrefetchScalarGridSpec(
            num_scalar_prefetch=1, grid=(), in_specs=[vmem] * 5, out_specs=vmem
        ),
        compiler_params=pltpu.CompilerParams(vmem_limit_bytes=24 << 20),
        cost_estimate=pl.CostEstimate(flops=1 << 20, bytes_accessed=6 << 20, transcendentals=0),
        name="join",
    )(place, d00, d01, d10, d11, mirror)


def on_device(coeffs, hamiltonian_tiles, source_lists, present):
    xl, core, y = (lax.axis_index(a).astype(jnp.int32) for a in ("xl", "core", "y"))
    matrices = hamiltonian_tiles[0]

    small = jnp.concatenate([source_lists[0], present.reshape(-1)]).astype(jnp.int32)
    pair = jnp.stack([small, lax.ppermute(small, "core", SWAP)])
    four = jnp.concatenate([pair, lax.ppermute(pair, "xl", SWAP)])

    slots = coeffs.reshape(2, 2, HALF, T)

    def piece(slot, half):
        return lax.dynamic_slice(slots, (slot, half, 0, 0), (1, 1, HALF, T)).reshape(HALF, T)

    other_slot = lax.dynamic_slice(slots, (1 - core, 0, 0, 0), (1, 2, HALF, T))[0]
    from_core = lax.ppermute(other_slot, "core", SWAP)
    near = [piece(core, xl), lax.dynamic_slice(from_core, (xl, 0, 0), (1, HALF, T))[0]]
    send = [piece(core, 1 - xl), lax.dynamic_slice(from_core, (1 - xl, 0, 0), (1, HALF, T))[0]]
    local = near + [lax.ppermute(s, "xl", SWAP) for s in send]
    tiles = list(local)
    by_step = {}
    for i, block in enumerate(local):
        for dy in (1, 3, 2):
            by_step[dy, i] = lax.ppermute(block, "y", along_y(-dy % 4))
    for dy in (1, 2, 3):
        tiles += [by_step[dy, i] for i in range(4)]

    core_m = lax.ppermute(matrices, "core", SWAP)
    far = [lax.ppermute(matrices[m], ("xh", "xl"), OUTER) for m in range(3)]
    far.append(lax.ppermute(matrices[3], "xl", SWAP))
    far += [lax.ppermute(f, "core", SWAP) for f in far]

    column = y * 4 + xl * 2 + core
    own = jnp.stack([column, column ^ 1, column ^ 2, column ^ 3])
    sources = jnp.concatenate([own[:, None], four[:, :3]], axis=1)
    place = ((sources // 4 - y) % 4) * 4 + ((sources ^ column) & 3)
    where = jnp.stack([xl, core])
    table = jnp.concatenate([place.reshape(-1), where])
    mask = four[:, 3:].reshape(-1)

    mirror, near_sum, far_sum = half_products(table, mask, tiles, matrices, core_m, far)

    from_far = lax.ppermute(far_sum, "xl", SWAP)
    d10 = lax.ppermute(near_sum[1], "core", SWAP)
    d11 = lax.ppermute(from_far[1], "core", SWAP)

    spread = lax.all_to_all(
        mirror.reshape(32, 32, T), ("xh", "z", "y"), split_axis=0, concat_axis=0, tiled=True
    )
    spread = spread.reshape(2, 2, 2, 2, 2, 2, 16, T).transpose(3, 4, 5, 0, 1, 2, 6, 7)
    owned = lax.all_to_all(
        spread.reshape(64, 16, T), ("xh", "z", "y", "xl"), split_axis=0, concat_axis=0, tiled=True
    )
    return join(where, near_sum[0], from_far[0], d10, d11, owned.reshape(32, 2, 2, 8, T))


def solution(mesh):
    fine = Mesh(mesh.devices.reshape(SIZES), AXES)
    row, col = ("xh", "z"), ("y", "xl", "core")
    placed = (P(row, col), P(col, None, None, None), P(col, None), P(col, None, None, None))
    return jax.shard_map(on_device, mesh=fine, in_specs=placed, out_specs=P(row, col), check_vma=False)
```

```python
import jax
import jax.numpy as jnp
from jax import lax
from jax.experimental import pallas as pl
from jax.experimental.pallas import tpu as pltpu
from jax.sharding import Mesh, PartitionSpec as P


SIZES = (2, 4, 4, 2, 2)
AXES = ("xh", "z", "y", "xl", "core")
T = 512
HALF = 256
B = 128

SWAP = [(0, 1), (1, 0)]
OUTER = [(0, 3), (3, 0), (1, 2), (2, 1)]


def along_y(step):
    return [(i, (i + step) % 4) for i in range(4)]


def split(value):
    high = value.astype(jnp.bfloat16)
    return high, (value - high.astype(jnp.float32)).astype(jnp.bfloat16)


def dot(left, right):
    return jnp.dot(left, right, preferred_element_type=jnp.float32)


def product_kernel(columns, loaded, wanted, sources, targets, only_held, refs):
    table, mask = refs["table"], refs["mask"]
    c_all, m_all, acc, arrived, c_sem, m_sem, s_sem, o_sem = refs["scratch"]

    def wants(jm):
        return wanted(jm // 4, jm % 4, table[jm])

    def when_held(j):
        if not only_held:
            return lambda f: f()
        found = wants(j * 4)
        for m in range(1, 4):
            found = jnp.logical_or(found, wants(j * 4 + m))
        return pl.when(found)

    def fetch(j):
        source = sources(refs, j)
        return [] if source is None else [pltpu.make_async_copy(source, acc.at[j], s_sem.at[j])]

    def put(j):
        return [
            pltpu.make_async_copy(acc.at[j], target, o_sem.at[j, i])
            for i, target in enumerate(targets(refs, j))
        ]

    count = len(loaded)
    for i in range(count):
        arrived[i] = jnp.int32(0)
    bounds = [4] + [4 + (count - 4) * (n + 1) // len(columns) for n in range(len(columns))]
    bounds = [min(b, count) for b in bounds]

    def tile_copy(i):
        return pltpu.make_async_copy(refs["tiles"][i], c_all.at[i], c_sem.at[i])

    for i in range(bounds[0]):
        tile_copy(i).start()
    for n, j in enumerate(columns):

        @when_held(j)
        def _(j=j):
            if sources(refs, j) is None:
                acc[j] = jnp.zeros(acc.shape[1:], jnp.float32)
            for copy in fetch(j):
                copy.start()

        for m in range(4):

            @pl.when(wants(j * 4 + m))
            def _(j=j, m=m):
                start = 0
                for part, size, chosen in refs["matrix"][j][m]:
                    there = m_all.at[j * 4 + m, pl.ds(start, size), :]
                    copy = pltpu.make_async_copy(part, there, m_sem.at[j * 4 + m])
                    if chosen is None:
                        copy.start()
                        start += size
                    else:
                        at, value, last = chosen
                        pl.when(at == value)(copy.start)
                        start += size if last else 0

        for i in range(bounds[n], bounds[n + 1]):
            tile_copy(i).start()
    for j in columns:

        @when_held(j)
        def _(j=j):
            for copy in fetch(j):
                copy.wait()

    def pair(jm, carry):
        @pl.when(wants(jm))
        def _():
            pltpu.make_async_copy(refs["matrix"][0][0][0][0], m_all.at[jm], m_sem.at[jm]).wait()
            at = jnp.int32(0)
            for i, tile in enumerate(loaded):
                at = jnp.where(table[jm] == tile, i, at)

            @pl.when(arrived[at] == 0)
            def _():
                pltpu.make_async_copy(refs["tiles"][0], c_all.at[at], c_sem.at[at]).wait()
                arrived[at] = jnp.int32(1)

            left_high, left_low = split(c_all[at])
            bands = []
            for bi in range(4):
                flags = [
                    jnp.full((1, B), mask[jm * 16 + bi * 4 + bj].astype(jnp.float32), jnp.float32)
                    for bj in range(4)
                ]
                bands.append(m_all[jm, bi * B : (bi + 1) * B, :] * jnp.concatenate(flags, axis=1))
            high, low = split(jnp.concatenate(bands, axis=0))
            total = dot(left_high, high) + (dot(left_high, low) + dot(left_low, high))
            acc[jm // 4] = acc[jm // 4] + total.reshape(32, 8, T)

        return carry

    lax.fori_loop(columns[0] * 4, columns[-1] * 4 + 4, pair, 0)
    for i in range(count):

        @pl.when(arrived[i] == 0)
        def _(i=i):
            tile_copy(i).wait()

    for act in ("start", "wait"):
        for j in columns:

            @when_held(j)
            def _(j=j, act=act):
                for copy in put(j):
                    getattr(copy, act)()


SUMS = jax.ShapeDtypeStruct((2, 32, 8, T), jnp.float32)
MIRROR = jax.ShapeDtypeStruct((32, 2, 2, 8, T), jnp.float32)
EARLY = (0, 1, 2, 3, 4, 5, 6, 12, 13, 14)
REST = (7, 15, 8, 9)
LAST = (10, 11)


def one_of(t, ids):
    found = t == ids[0]
    for i in ids[1:]:
        found = jnp.logical_or(found, t == i)
    return found


def sum_refs(refs, j):
    return refs["sums"][j // 2].at[j % 2]


def sum_and_mirror(refs, j):
    xl, core = refs["table"][16], refs["table"][17]
    return [
        sum_refs(refs, j),
        refs["mirror"].at[:, (xl + j // 2) % 2, (core + j % 2) % 2],
    ]


def products(table, mask, tiles, matrix, before, columns, loaded, wanted, outs, only_held, flops):
    parts = [part[0] for j in matrix for slot in j for part in slot]
    flat, index = [], {}
    for part in parts:
        if id(part) not in index:
            index[id(part)] = len(flat)
            flat.append(part)

    def kernel(table_ref, mask_ref, *refs):
        refs = list(refs)
        tile_refs = [refs.pop(0) for _ in tiles]
        flat_refs = [refs.pop(0) for _ in flat]
        before_refs = [refs.pop(0) for _ in before]
        out_refs = [refs.pop(0) for _ in outs]

        def look(part, where, chosen=None):
            ref = flat_refs[index[id(part)]]
            if part.ndim == 3:
                return ref.at[where], T, None
            if chosen is not None:
                chosen = ((chosen[0] - table_ref[18]) & 3, chosen[1], chosen[2])
            return ref.at[pl.ds(*where)], where[1], chosen

        named = {
            "table": table_ref,
            "mask": mask_ref,
            "tiles": tile_refs,
            "matrix": [[[look(*p) for p in slot] for slot in j] for j in matrix],
            "before": before_refs,
            "sums": out_refs[:2],
            "mirror": out_refs[2] if len(outs) > 2 else None,
            "scratch": refs,
        }

        def sources(r, j):
            if only_held:
                return sum_refs(r, j)
            return r["before"][j // 2].at[j % 2] if len(before) > j // 2 else None

        def targets(r, j):
            return sum_and_mirror(r, j) if r["mirror"] is not None else [sum_refs(r, j)]

        product_kernel(columns, loaded, wanted, sources, targets, only_held, named)

    inputs = len(tiles) + len(flat) + len(before)
    anywhere = pl.BlockSpec(memory_space=pltpu.HBM)
    aliases = {2 + len(tiles) + len(flat) + i: i for i in range(len(outs))} if only_held else {}
    return pl.pallas_call(
        kernel,
        out_shape=tuple(outs),
        grid_spec=pltpu.PrefetchScalarGridSpec(
            num_scalar_prefetch=2,
            grid=(),
            in_specs=[anywhere] * inputs,
            out_specs=tuple([anywhere] * len(outs)),
            scratch_shapes=[
                pltpu.VMEM((len(loaded), HALF, T), jnp.float32),
                pltpu.VMEM((4 * len(columns), T, T), jnp.float32),
                pltpu.VMEM((len(columns), 32, 8, T), jnp.float32),
                pltpu.SMEM((16,), jnp.int32),
                pltpu.SemaphoreType.DMA((len(loaded),)),
                pltpu.SemaphoreType.DMA((16,)),
                pltpu.SemaphoreType.DMA((4,)),
                pltpu.SemaphoreType.DMA((4, 2)),
            ],
        ),
        input_output_aliases=aliases,
        compiler_params=pltpu.CompilerParams(vmem_limit_bytes=60 << 20),
        cost_estimate=pl.CostEstimate(flops=flops, bytes_accessed=8 << 20, transcendentals=0),
    )(table, mask, *tiles, *flat, *before)


def join_kernel(place, d00, d01, d10, d11, mirror, out, parts, sems):
    xl, core = place[0], place[1]
    pieces = (d00, d01, d10, d11)
    copies = [pltpu.make_async_copy(p, parts.at[i], sems.at[i]) for i, p in enumerate(pieces)]
    for copy in copies:
        copy.start()
    for i, copy in enumerate(copies):
        copy.wait()
        slot = (core + i // 2) % 2
        half = (xl + i % 2) % 2
        columns = pl.ds(pl.multiple_of(half * HALF, HALF), HALF)
        rows = pl.ds(pl.multiple_of((slot * 2 + half) * HALF, HALF), HALF)
        for h in range(2):
            turned = mirror[:, h, slot, :, columns].reshape(HALF, HALF).T
            out[rows, h * HALF : (h + 1) * HALF] = parts[i, :, h * HALF : (h + 1) * HALF] + turned


def join(place, d00, d01, d10, d11, mirror):
    vmem = pl.BlockSpec(memory_space=pltpu.VMEM)
    anywhere = pl.BlockSpec(memory_space=pltpu.HBM)
    return pl.pallas_call(
        join_kernel,
        out_shape=jax.ShapeDtypeStruct((2 * T, T), jnp.float32),
        grid_spec=pltpu.PrefetchScalarGridSpec(
            num_scalar_prefetch=1,
            grid=(),
            in_specs=[anywhere] * 4 + [vmem],
            out_specs=vmem,
            scratch_shapes=[
                pltpu.VMEM((4, HALF, T), jnp.float32),
                pltpu.SemaphoreType.DMA((4,)),
            ],
        ),
        compiler_params=pltpu.CompilerParams(vmem_limit_bytes=24 << 20),
        cost_estimate=pl.CostEstimate(flops=1 << 20, bytes_accessed=6 << 20, transcendentals=0),
        name="join",
    )(place, d00, d01, d10, d11, mirror)


def on_device(coeffs, hamiltonian_tiles, source_lists, present):
    xl, core, y, z = (lax.axis_index(a).astype(jnp.int32) for a in ("xl", "core", "y", "z"))
    matrices = hamiltonian_tiles[0]

    small = jnp.concatenate([source_lists[0], present.reshape(-1)]).astype(jnp.int32)
    both = [(i, 3 - i) for i in range(4)]
    four = jnp.stack(
        [
            small,
            lax.ppermute(small, "core", SWAP),
            lax.ppermute(small, "xl", SWAP),
            lax.ppermute(small, ("xl", "core"), both),
        ]
    )

    slots = coeffs.reshape(2, 2, HALF, T)

    def piece(slot, half):
        return lax.dynamic_slice(slots, (slot, half, 0, 0), (1, 1, HALF, T)).reshape(HALF, T)

    other_slot = lax.dynamic_slice(slots, (1 - core, 0, 0, 0), (1, 2, HALF, T))[0]
    from_core = lax.ppermute(other_slot, "core", SWAP)
    near = [piece(core, xl), lax.dynamic_slice(from_core, (xl, 0, 0), (1, HALF, T))[0]]
    send = [piece(core, 1 - xl), lax.dynamic_slice(from_core, (1 - xl, 0, 0), (1, HALF, T))[0]]
    local = near + [lax.ppermute(s, "xl", SWAP) for s in send]
    up = [lax.ppermute(t, "y", along_y(1)) for t in local]
    down = [lax.ppermute(t, "y", along_y(-1)) for t in local]
    onward = [lax.ppermute((up, down)[i % 2][i], "y", along_y((1, -1)[i % 2])) for i in range(4)]
    tiles = local + down + onward + up

    core_m = lax.ppermute(matrices, "core", SWAP)
    strips = matrices.reshape(4 * T, T)
    cut_z = lax.dynamic_slice(strips, (2 * T + z * HALF, 0), (HALF, T))
    cut_a, cut_b = matrices[0], matrices[1]
    far_a = lax.ppermute(cut_a, ("xh", "xl"), OUTER)
    far_b = lax.ppermute(cut_b, "xl", SWAP)
    near_z = lax.ppermute(cut_z, ("xh", "xl"), OUTER)
    far_z = [
        near_z,
        lax.ppermute(near_z, "z", along_y(-1)),
        lax.ppermute(near_z, "z", along_y(2)),
        lax.ppermute(near_z, "z", along_y(1)),
    ]
    far = [far_a, far_b] + far_z
    farther = [lax.ppermute(cut, "core", SWAP) for cut in far]

    def quarter(q, pieces):
        return [(p, (0, HALF), (q, step, step == 3)) for step, p in enumerate(pieces)]

    matrix = [[[(m, slot)] for slot in range(4)] for m in (matrices, core_m)]
    matrix += [
        [[(f[0], (0, T))], [(f[1], (0, T))]]
        + [quarter(2 * s, f[2:]) + quarter(2 * s + 1, f[2:]) for s in range(2)]
        for f in (far, farther)
    ]

    column = y * 4 + xl * 2 + core
    own = jnp.stack([column, column ^ 1, column ^ 2, column ^ 3])
    sources = jnp.concatenate([own[:, None], four[:, :3]], axis=1)
    place = ((sources // 4 - y) % 4) * 4 + ((sources ^ column) & 3)
    where = jnp.stack([xl, core, z])
    table = jnp.concatenate([place.reshape(-1), where])
    mask = four[:, 3:].reshape(-1)

    unit = 6 * HALF * T * T

    def pick(ids):
        return [tiles[i] for i in ids]

    def in_later(j, m, t):
        return jnp.where(j < 2, one_of(t, REST), jnp.logical_not(one_of(t, LAST)))

    four_columns = (0, 1, 2, 3)
    sums = products(
        table, mask, pick(EARLY), matrix[:2], [], (0, 1), EARLY,
        lambda j, m, t: one_of(t, EARLY), [SUMS], False, 5 * unit,
    )
    later = EARLY + REST
    sums = products(
        table, mask, pick(later), matrix, sums, four_columns, later,
        in_later, [SUMS, SUMS, MIRROR], False, 9 * unit,
    )
    near_sum, far_sum, mirror = products(
        table, mask, pick(LAST), matrix, sums, four_columns, LAST,
        lambda j, m, t: one_of(t, LAST), [SUMS, SUMS, MIRROR], True, 2 * unit,
    )
    near_sum, far_sum = (m.reshape(2, HALF, T) for m in (near_sum, far_sum))

    from_far = lax.ppermute(far_sum, "xl", SWAP)
    d10 = lax.ppermute(near_sum[1], "core", SWAP)
    d11 = lax.ppermute(from_far[1], "core", SWAP)

    spread = lax.all_to_all(
        mirror.reshape(32, 32, T), ("xh", "z", "y"), split_axis=0, concat_axis=0, tiled=True
    )
    spread = spread.reshape(2, 2, 2, 2, 2, 2, 16, T).transpose(3, 4, 5, 0, 1, 2, 6, 7)
    owned = lax.all_to_all(
        spread.reshape(64, 16, T), ("xh", "z", "y", "xl"), split_axis=0, concat_axis=0, tiled=True
    )
    return join(where, near_sum[0], from_far[0], d10, d11, owned.reshape(32, 2, 2, 8, T))


def solution(mesh):
    fine = Mesh(mesh.devices.reshape(SIZES), AXES)
    row, col = ("xh", "z"), ("y", "xl", "core")
    placed = (P(row, col), P(col, None, None, None), P(col, None), P(col, None, None, None))

    return jax.shard_map(on_device, mesh=fine, in_specs=placed, out_specs=P(row, col), check_vma=False)
```

```python
import jax
import jax.numpy as jnp
from jax import lax
from jax.experimental import pallas as pl
from jax.experimental.pallas import tpu as pltpu
from jax.sharding import Mesh, PartitionSpec as P


SIZES = (2, 4, 4, 2, 2)
AXES = ("xh", "z", "y", "xl", "core")
T = 512
HALF = 256
B = 128

SWAP = [(0, 1), (1, 0)]
OUTER = [(0, 3), (3, 0), (1, 2), (2, 1)]


def along_y(step):
    return [(i, (i + step) % 4) for i in range(4)]


def split(value):
    high = value.astype(jnp.bfloat16)
    return high, (value - high.astype(jnp.float32)).astype(jnp.bfloat16)


def dot(left, right):
    return jnp.dot(left, right, preferred_element_type=jnp.float32)


def product_kernel(columns, loaded, wanted, sources, targets, only_held, refs):
    table, mask = refs["table"], refs["mask"]
    c_all, m_all, acc, left, right, arrived, c_sem, m_sem, s_sem, o_sem = refs["scratch"]

    def wants(jm):
        return wanted(jm // 4, jm % 4, table[jm])

    def when_held(j):
        if not only_held:
            return lambda f: f()
        found = wants(j * 4)
        for m in range(1, 4):
            found = jnp.logical_or(found, wants(j * 4 + m))
        return pl.when(found)

    def fetch(j):
        source = sources(refs, j)
        return [] if source is None else [pltpu.make_async_copy(source, acc.at[j], s_sem.at[j])]

    def put(j):
        return [
            pltpu.make_async_copy(acc.at[j], target, o_sem.at[j, i])
            for i, target in enumerate(targets(refs, j))
        ]

    count = len(loaded)
    for i in range(count):
        arrived[i] = jnp.int32(0)
    bounds = [4] + [4 + (count - 4) * (n + 1) // len(columns) for n in range(len(columns))]
    bounds = [min(b, count) for b in bounds]

    def tile_copy(i):
        return pltpu.make_async_copy(refs["tiles"][i], c_all.at[i], c_sem.at[i])

    for i in range(bounds[0]):
        tile_copy(i).start()
    for n, j in enumerate(columns):

        @when_held(j)
        def _(j=j):
            if sources(refs, j) is None:
                acc[j] = jnp.zeros(acc.shape[1:], jnp.float32)
            for copy in fetch(j):
                copy.start()

        for m in range(4):

            @pl.when(wants(j * 4 + m))
            def _(j=j, m=m):
                start = 0
                for part, size, chosen in refs["matrix"][j][m]:
                    there = m_all.at[j * 4 + m, pl.ds(start, size), :]
                    copy = pltpu.make_async_copy(part, there, m_sem.at[j * 4 + m])
                    if chosen is None:
                        copy.start()
                        start += size
                    else:
                        at, value, last = chosen
                        pl.when(at == value)(copy.start)
                        start += size if last else 0

        for i in range(bounds[n], bounds[n + 1]):
            tile_copy(i).start()
    for j in columns:

        @when_held(j)
        def _(j=j):
            for copy in fetch(j):
                copy.wait()

    def pair(jm, carry):
        @pl.when(wants(jm))
        def _():
            pltpu.make_async_copy(refs["matrix"][0][0][0][0], m_all.at[jm], m_sem.at[jm]).wait()
            at = jnp.int32(0)
            for i, tile in enumerate(loaded):
                at = jnp.where(table[jm] == tile, i, at)

            @pl.when(arrived[at] == 0)
            def _():
                pltpu.make_async_copy(refs["tiles"][0], c_all.at[at], c_sem.at[at]).wait()
                arrived[at] = jnp.int32(1)

            left[:, :T], left[:, T : 2 * T] = split(c_all[at])
            left[:, 2 * T :] = left[:, :T]
            for bi in range(4):
                flags = [
                    jnp.full((1, B), mask[jm * 16 + bi * 4 + bj].astype(jnp.float32), jnp.float32)
                    for bj in range(4)
                ]
                rows = slice(bi * B, (bi + 1) * B)
                high, low = split(m_all[jm, rows, :] * jnp.concatenate(flags, axis=1))
                right[bi * B : (bi + 1) * B, :] = high
                right[T + bi * B : T + (bi + 1) * B, :] = high
                right[2 * T + bi * B : 2 * T + (bi + 1) * B, :] = low
            acc[jm // 4] = acc[jm // 4] + dot(left[...], right[...]).reshape(32, 8, T)

        return carry

    lax.fori_loop(columns[0] * 4, columns[-1] * 4 + 4, pair, 0)
    for i in range(count):

        @pl.when(arrived[i] == 0)
        def _(i=i):
            tile_copy(i).wait()

    for act in ("start", "wait"):
        for j in columns:

            @when_held(j)
            def _(j=j, act=act):
                for copy in put(j):
                    getattr(copy, act)()


SUM = jax.ShapeDtypeStruct((32, 8, T), jnp.float32)
MIRROR = jax.ShapeDtypeStruct((32, 2, 2, 8, T), jnp.float32)
EARLY = (0, 1, 2, 3, 4, 5, 12, 13)
MIDDLE = (6, 14, 7, 15)
LATE = (8, 9)
LAST = (10, 11)


def one_of(t, ids):
    found = t == ids[0]
    for i in ids[1:]:
        found = jnp.logical_or(found, t == i)
    return found


def sum_refs(refs, j):
    return refs["sums"][j]


def sum_and_mirror(refs, j):
    xl, core = refs["table"][16], refs["table"][17]
    return [
        sum_refs(refs, j),
        refs["mirror"].at[:, (xl + j // 2) % 2, (core + j % 2) % 2],
    ]


def products(table, mask, tiles, matrix, before, columns, loaded, wanted, outs, only_held, flops):
    parts = [part[0] for j in matrix for slot in j for part in slot]
    flat, index = [], {}
    for part in parts:
        if id(part) not in index:
            index[id(part)] = len(flat)
            flat.append(part)

    def kernel(table_ref, mask_ref, *refs):
        refs = list(refs)
        tile_refs = [refs.pop(0) for _ in tiles]
        flat_refs = [refs.pop(0) for _ in flat]
        before_refs = [refs.pop(0) for _ in before]
        out_refs = [refs.pop(0) for _ in outs]

        def look(part, where, chosen=None):
            ref = flat_refs[index[id(part)]]
            if part.ndim == 3:
                return ref.at[where], T, None
            if chosen is not None:
                chosen = ((chosen[0] - table_ref[18]) & 3, chosen[1], chosen[2])
            return ref.at[pl.ds(*where)], where[1], chosen

        named = {
            "table": table_ref,
            "mask": mask_ref,
            "tiles": tile_refs,
            "matrix": [[[look(*p) for p in slot] for slot in j] for j in matrix],
            "before": before_refs,
            "sums": out_refs[:4],
            "mirror": out_refs[4] if len(outs) > 4 else None,
            "scratch": refs,
        }

        def sources(r, j):
            if only_held:
                return sum_refs(r, j)
            return r["before"][j] if len(before) > j else None

        def targets(r, j):
            return sum_and_mirror(r, j) if r["mirror"] is not None else [sum_refs(r, j)]

        product_kernel(columns, loaded, wanted, sources, targets, only_held, named)

    inputs = len(tiles) + len(flat) + len(before)
    anywhere = pl.BlockSpec(memory_space=pltpu.HBM)
    aliases = {2 + len(tiles) + len(flat) + i: i for i in range(len(outs))} if only_held else {}
    return pl.pallas_call(
        kernel,
        out_shape=tuple(outs),
        grid_spec=pltpu.PrefetchScalarGridSpec(
            num_scalar_prefetch=2,
            grid=(),
            in_specs=[anywhere] * inputs,
            out_specs=tuple([anywhere] * len(outs)),
            scratch_shapes=[
                pltpu.VMEM((len(loaded), HALF, T), jnp.float32),
                pltpu.VMEM((4 * len(columns), T, T), jnp.float32),
                pltpu.VMEM((len(columns), 32, 8, T), jnp.float32),
                pltpu.VMEM((HALF, 3 * T), jnp.bfloat16),
                pltpu.VMEM((3 * T, T), jnp.bfloat16),
                pltpu.SMEM((16,), jnp.int32),
                pltpu.SemaphoreType.DMA((len(loaded),)),
                pltpu.SemaphoreType.DMA((16,)),
                pltpu.SemaphoreType.DMA((4,)),
                pltpu.SemaphoreType.DMA((4, 2)),
            ],
        ),
        input_output_aliases=aliases,
        compiler_params=pltpu.CompilerParams(vmem_limit_bytes=60 << 20),
        cost_estimate=pl.CostEstimate(flops=flops, bytes_accessed=8 << 20, transcendentals=0),
    )(table, mask, *tiles, *flat, *before)


def assemble_kernel(place, d00, d01, d10, d11, out, sems):
    xl, core = place[0], place[1]
    copies = []
    for i, piece in enumerate((d00, d01, d10, d11)):
        block = (core + i // 2) % 2 * 2 + (xl + i % 2) % 2
        rows = pl.ds(pl.multiple_of(block * HALF, HALF), HALF)
        copies.append(pltpu.make_async_copy(piece, out.at[rows], sems.at[i]))
        copies[-1].start()
    for copy in copies:
        copy.wait()


def assemble(place, d00, d01, d10, d11):
    return pl.pallas_call(
        assemble_kernel,
        out_shape=jax.ShapeDtypeStruct((2 * T, T), jnp.float32),
        grid_spec=pltpu.PrefetchScalarGridSpec(
            num_scalar_prefetch=1,
            grid=(),
            in_specs=[pl.BlockSpec(memory_space=pl.ANY)] * 4,
            out_specs=pl.BlockSpec(memory_space=pltpu.VMEM),
            scratch_shapes=[pltpu.SemaphoreType.DMA((4,))],
        ),
        compiler_params=pltpu.CompilerParams(vmem_limit_bytes=8 << 20),
        cost_estimate=pl.CostEstimate(flops=0, bytes_accessed=4 << 20, transcendentals=0),
        name="assemble",
    )(place, d00, d01, d10, d11)


def join_kernel(direct, mirror, out):
    for slot in range(2):
        for half in range(2):
            for h in range(2):
                rows = slice((slot * 2 + half) * HALF, (slot * 2 + half + 1) * HALF)
                columns = slice(h * HALF, (h + 1) * HALF)
                turned = mirror[:, h, slot, :, half * HALF : (half + 1) * HALF]
                out[rows, columns] = direct[rows, columns] + turned.reshape(HALF, HALF).T


def join(direct, mirror):
    vmem = pl.BlockSpec(memory_space=pltpu.VMEM)
    return pl.pallas_call(
        join_kernel,
        out_shape=jax.ShapeDtypeStruct((2 * T, T), jnp.float32),
        in_specs=[vmem] * 2,
        out_specs=vmem,
        compiler_params=pltpu.CompilerParams(vmem_limit_bytes=24 << 20),
        cost_estimate=pl.CostEstimate(flops=1 << 20, bytes_accessed=6 << 20, transcendentals=0),
        name="join",
    )(direct, mirror)


def on_device(coeffs, hamiltonian_tiles, source_lists, present):
    xl, core, y, z = (lax.axis_index(a).astype(jnp.int32) for a in ("xl", "core", "y", "z"))
    matrices = hamiltonian_tiles[0]

    small = jnp.concatenate([source_lists[0], present.reshape(-1)]).astype(jnp.int32)
    both = [(i, 3 - i) for i in range(4)]
    four = jnp.stack(
        [
            small,
            lax.ppermute(small, "core", SWAP),
            lax.ppermute(small, "xl", SWAP),
            lax.ppermute(small, ("xl", "core"), both),
        ]
    )

    slots = coeffs.reshape(2, 2, HALF, T)

    def piece(slot, half):
        return lax.dynamic_slice(slots, (slot, half, 0, 0), (1, 1, HALF, T)).reshape(HALF, T)

    other_slot = lax.dynamic_slice(slots, (1 - core, 0, 0, 0), (1, 2, HALF, T))[0]
    from_core = lax.ppermute(other_slot, "core", SWAP)
    near = [piece(core, xl), lax.dynamic_slice(from_core, (xl, 0, 0), (1, HALF, T))[0]]
    send = [piece(core, 1 - xl), lax.dynamic_slice(from_core, (1 - xl, 0, 0), (1, HALF, T))[0]]
    local = near + [lax.ppermute(s, "xl", SWAP) for s in send]
    up = [lax.ppermute(t, "y", along_y(1)) for t in local]
    down = [lax.ppermute(t, "y", along_y(-1)) for t in local]
    onward = [lax.ppermute((up, down)[i % 2][i], "y", along_y((1, -1)[i % 2])) for i in range(4)]
    tiles = local + down + onward + up

    core_m = lax.ppermute(matrices, "core", SWAP)
    strips = matrices.reshape(4 * T, T)
    cut_z = lax.dynamic_slice(strips, (2 * T + z * HALF, 0), (HALF, T))
    cut_a, cut_b = matrices[0], matrices[1]
    far_a = lax.ppermute(cut_a, ("xh", "xl"), OUTER)
    far_b = lax.ppermute(cut_b, "xl", SWAP)
    near_z = lax.ppermute(cut_z, ("xh", "xl"), OUTER)
    far_z = [
        near_z,
        lax.ppermute(near_z, "z", along_y(-1)),
        lax.ppermute(near_z, "z", along_y(2)),
        lax.ppermute(near_z, "z", along_y(1)),
    ]
    far = [far_a, far_b] + far_z
    farther = [lax.ppermute(cut, "core", SWAP) for cut in far]

    def quarter(q, pieces):
        return [(p, (0, HALF), (q, step, step == 3)) for step, p in enumerate(pieces)]

    matrix = [[[(m, slot)] for slot in range(4)] for m in (matrices, core_m)]
    matrix += [
        [[(f[0], (0, T))], [(f[1], (0, T))]]
        + [quarter(2 * s, f[2:]) + quarter(2 * s + 1, f[2:]) for s in range(2)]
        for f in (far, farther)
    ]

    column = y * 4 + xl * 2 + core
    own = jnp.stack([column, column ^ 1, column ^ 2, column ^ 3])
    sources = jnp.concatenate([own[:, None], four[:, :3]], axis=1)
    place = ((sources // 4 - y) % 4) * 4 + ((sources ^ column) & 3)
    where = jnp.stack([xl, core, z])
    table = jnp.concatenate([place.reshape(-1), where])
    mask = four[:, 3:].reshape(-1)

    unit = 6 * HALF * T * T

    def pick(ids):
        return [tiles[i] for i in ids]

    def in_middle(j, m, t):
        return jnp.where(j < 2, one_of(t, MIDDLE), jnp.logical_not(one_of(t, LATE + LAST)))

    four_columns = (0, 1, 2, 3)
    sums = products(
        table, mask, pick(EARLY), matrix[:2], [], (0, 1), EARLY,
        lambda j, m, t: one_of(t, EARLY), [SUM] * 2, False, 5 * unit,
    )
    sums = products(
        table, mask, pick(EARLY + MIDDLE), matrix, sums, four_columns, EARLY + MIDDLE,
        in_middle, [SUM] * 4 + [MIRROR], False, 8 * unit,
    )
    for ids in (LATE, LAST):
        sums = products(
            table, mask, pick(ids), matrix, sums, four_columns, ids,
            lambda j, m, t, ids=ids: one_of(t, ids), [SUM] * 4 + [MIRROR], True, 2 * unit,
        )
    mirror = sums[4]
    near, core_near, far_near, far_core = (m.reshape(HALF, T) for m in sums[:4])
    d01 = lax.ppermute(far_near, "xl", SWAP)
    from_far = lax.ppermute(far_core, "xl", SWAP)
    d10 = lax.ppermute(core_near, "core", SWAP)
    d11 = lax.ppermute(from_far, "core", SWAP)

    spread = lax.all_to_all(
        mirror.reshape(32, 32, T), ("xh", "z", "y"), split_axis=0, concat_axis=0, tiled=True
    )
    spread = spread.reshape(2, 2, 2, 2, 2, 2, 16, T).transpose(3, 4, 5, 0, 1, 2, 6, 7)
    owned = lax.all_to_all(
        spread.reshape(64, 16, T), ("xh", "z", "y", "xl"), split_axis=0, concat_axis=0, tiled=True
    )
    direct = assemble(where, near, d01, d10, d11)
    return join(direct, owned.reshape(32, 2, 2, 8, T))


def solution(mesh):
    fine = Mesh(mesh.devices.reshape(SIZES), AXES)
    row, col = ("xh", "z"), ("y", "xl", "core")
    placed = (P(row, col), P(col, None, None, None), P(col, None), P(col, None, None, None))

    return jax.shard_map(on_device, mesh=fine, in_specs=placed, out_specs=P(row, col), check_vma=False)
```

```python
import jax
import jax.numpy as jnp
from jax import lax
from jax.experimental import pallas as pl
from jax.experimental.pallas import tpu as pltpu
from jax.sharding import Mesh, PartitionSpec as P


SIZES = (2, 4, 4, 2, 2)
AXES = ("xh", "z", "y", "xl", "core")
T = 512
HALF = 256
B = 128

SWAP = [(0, 1), (1, 0)]
OUTER = [(0, 3), (3, 0), (1, 2), (2, 1)]


def along_y(step):
    return [(i, (i + step) % 4) for i in range(4)]


def split(value):
    high = value.astype(jnp.bfloat16)
    return high, (value - high.astype(jnp.float32)).astype(jnp.bfloat16)


def dot(left, right):
    return jnp.dot(left, right, preferred_element_type=jnp.float32)


def product_kernel(columns, loaded, wanted, sources, targets, only_held, refs):
    table = refs["table"]
    c_all, m_all, acc, left, right, arrived, c_sem, m_sem, s_sem, o_sem = refs["scratch"]

    def wants(jm):
        return wanted(jm // 4, jm % 4, table[jm])

    def when_held(j):
        if not only_held:
            return lambda f: f()
        found = wants(j * 4)
        for m in range(1, 4):
            found = jnp.logical_or(found, wants(j * 4 + m))
        return pl.when(found)

    def fetch(j):
        source = sources(refs, j)
        return [] if source is None else [pltpu.make_async_copy(source, acc.at[j], s_sem.at[j])]

    def put(j):
        return [
            pltpu.make_async_copy(acc.at[j], target, o_sem.at[j, i])
            for i, target in enumerate(targets(refs, j))
        ]

    count = len(loaded)
    for i in range(count):
        arrived[i] = jnp.int32(0)
    bounds = [4] + [4 + (count - 4) * (n + 1) // len(columns) for n in range(len(columns))]
    bounds = [min(b, count) for b in bounds]

    def tile_copy(i):
        return pltpu.make_async_copy(refs["tiles"][i], c_all.at[i], c_sem.at[i])

    for i in range(bounds[0]):
        tile_copy(i).start()
    for n, j in enumerate(columns):

        @when_held(j)
        def _(j=j):
            if sources(refs, j) is None:
                acc[j] = jnp.zeros(acc.shape[1:], jnp.float32)
            for copy in fetch(j):
                copy.start()

        for m in range(4):

            @pl.when(wants(j * 4 + m))
            def _(j=j, m=m):
                start = 0
                for part, size, chosen in refs["matrix"][j][m]:
                    there = m_all.at[j * 4 + m, pl.ds(start, size), :]
                    copy = pltpu.make_async_copy(part, there, m_sem.at[j * 4 + m])
                    if chosen is None:
                        copy.start()
                        start += size
                    else:
                        at, value, last = chosen
                        pl.when(at == value)(copy.start)
                        start += size if last else 0

        for i in range(bounds[n], bounds[n + 1]):
            tile_copy(i).start()
    for j in columns:

        @when_held(j)
        def _(j=j):
            for copy in fetch(j):
                copy.wait()

    def pair(jm, carry):
        @pl.when(wants(jm))
        def _():
            pltpu.make_async_copy(refs["matrix"][0][0][0][0], m_all.at[jm], m_sem.at[jm]).wait()
            at = jnp.int32(0)
            for i, tile in enumerate(loaded):
                at = jnp.where(table[jm] == tile, i, at)

            @pl.when(arrived[at] == 0)
            def _():
                pltpu.make_async_copy(refs["tiles"][0], c_all.at[at], c_sem.at[at]).wait()
                arrived[at] = jnp.int32(1)

            left[:, :T], left[:, T : 2 * T] = split(c_all[at])
            left[:, 2 * T :] = left[:, :T]
            for bi in range(4):
                flags = [
                    jnp.full((1, B), table[FLAGS + jm * 16 + bi * 4 + bj].astype(jnp.float32), jnp.float32)
                    for bj in range(4)
                ]
                rows = slice(bi * B, (bi + 1) * B)
                high, low = split(m_all[jm, rows, :] * jnp.concatenate(flags, axis=1))
                right[bi * B : (bi + 1) * B, :] = high
                right[T + bi * B : T + (bi + 1) * B, :] = high
                right[2 * T + bi * B : 2 * T + (bi + 1) * B, :] = low
            acc[jm // 4] = acc[jm // 4] + dot(left[...], right[...]).reshape(32, 8, T)

        return carry

    lax.fori_loop(columns[0] * 4, columns[-1] * 4 + 4, pair, 0)
    for i in range(count):

        @pl.when(arrived[i] == 0)
        def _(i=i):
            tile_copy(i).wait()

    for act in ("start", "wait"):
        for j in columns:

            @when_held(j)
            def _(j=j, act=act):
                for copy in put(j):
                    getattr(copy, act)()


FLAGS = 19
SUM = jax.ShapeDtypeStruct((32, 8, T), jnp.float32)
MIRROR = jax.ShapeDtypeStruct((32, 2, 2, 8, T), jnp.float32)
EARLY = (0, 1, 2, 3, 4, 5, 12, 13)
MIDDLE = (6, 14, 7, 15)
LATE = (8, 9)
LAST = (10, 11)


def one_of(t, ids):
    found = t == ids[0]
    for i in ids[1:]:
        found = jnp.logical_or(found, t == i)
    return found


def sum_refs(refs, j):
    return refs["sums"][j]


def sum_and_mirror(refs, j):
    xl, core = refs["table"][16], refs["table"][17]
    return [
        sum_refs(refs, j),
        refs["mirror"].at[:, (xl + j // 2) % 2, (core + j % 2) % 2],
    ]


def products(table, tiles, matrix, before, columns, loaded, wanted, outs, only_held, flops):
    parts = [part[0] for j in matrix for slot in j for part in slot]
    flat, index = [], {}
    for part in parts:
        if id(part) not in index:
            index[id(part)] = len(flat)
            flat.append(part)

    def kernel(table_ref, *refs):
        refs = list(refs)
        tile_refs = [refs.pop(0) for _ in tiles]
        flat_refs = [refs.pop(0) for _ in flat]
        before_refs = [refs.pop(0) for _ in before]
        out_refs = [refs.pop(0) for _ in outs]

        def look(part, where, chosen=None):
            ref = flat_refs[index[id(part)]]
            if part.ndim == 3:
                return ref.at[where], T, None
            if chosen is not None:
                chosen = ((chosen[0] - table_ref[18]) & 3, chosen[1], chosen[2])
            return ref.at[pl.ds(*where)], where[1], chosen

        named = {
            "table": table_ref,
            "tiles": tile_refs,
            "matrix": [[[look(*p) for p in slot] for slot in j] for j in matrix],
            "before": before_refs,
            "sums": out_refs[:4],
            "mirror": out_refs[4] if len(outs) > 4 else None,
            "scratch": refs,
        }

        def sources(r, j):
            if only_held:
                return sum_refs(r, j)
            return r["before"][j] if len(before) > j else None

        def targets(r, j):
            return sum_and_mirror(r, j) if r["mirror"] is not None else [sum_refs(r, j)]

        product_kernel(columns, loaded, wanted, sources, targets, only_held, named)

    inputs = len(tiles) + len(flat) + len(before)
    anywhere = pl.BlockSpec(memory_space=pltpu.HBM)
    aliases = {1 + len(tiles) + len(flat) + i: i for i in range(len(outs))} if only_held else {}
    return pl.pallas_call(
        kernel,
        out_shape=tuple(outs),
        grid_spec=pltpu.PrefetchScalarGridSpec(
            num_scalar_prefetch=1,
            grid=(),
            in_specs=[anywhere] * inputs,
            out_specs=tuple([anywhere] * len(outs)),
            scratch_shapes=[
                pltpu.VMEM((len(loaded), HALF, T), jnp.float32),
                pltpu.VMEM((4 * len(columns), T, T), jnp.float32),
                pltpu.VMEM((len(columns), 32, 8, T), jnp.float32),
                pltpu.VMEM((HALF, 3 * T), jnp.bfloat16),
                pltpu.VMEM((3 * T, T), jnp.bfloat16),
                pltpu.SMEM((16,), jnp.int32),
                pltpu.SemaphoreType.DMA((len(loaded),)),
                pltpu.SemaphoreType.DMA((16,)),
                pltpu.SemaphoreType.DMA((4,)),
                pltpu.SemaphoreType.DMA((4, 2)),
            ],
        ),
        input_output_aliases=aliases,
        compiler_params=pltpu.CompilerParams(vmem_limit_bytes=60 << 20),
        cost_estimate=pl.CostEstimate(flops=flops, bytes_accessed=8 << 20, transcendentals=0),
    )(table, *tiles, *flat, *before)


def assemble_kernel(place, d00, d01, d10, d11, out, sems):
    xl, core = place[0], place[1]
    copies = []
    for i, piece in enumerate((d00, d01, d10, d11)):
        block = (core + i // 2) % 2 * 2 + (xl + i % 2) % 2
        rows = pl.ds(pl.multiple_of(block * HALF, HALF), HALF)
        copies.append(pltpu.make_async_copy(piece, out.at[rows], sems.at[i]))
        copies[-1].start()
    for copy in copies:
        copy.wait()


def assemble(place, d00, d01, d10, d11):
    return pl.pallas_call(
        assemble_kernel,
        out_shape=jax.ShapeDtypeStruct((2 * T, T), jnp.float32),
        grid_spec=pltpu.PrefetchScalarGridSpec(
            num_scalar_prefetch=1,
            grid=(),
            in_specs=[pl.BlockSpec(memory_space=pl.ANY)] * 4,
            out_specs=pl.BlockSpec(memory_space=pltpu.VMEM),
            scratch_shapes=[pltpu.SemaphoreType.DMA((4,))],
        ),
        compiler_params=pltpu.CompilerParams(vmem_limit_bytes=8 << 20),
        cost_estimate=pl.CostEstimate(flops=0, bytes_accessed=4 << 20, transcendentals=0),
        name="assemble",
    )(place, d00, d01, d10, d11)


def join_kernel(direct, mirror, out, held, sems, out_sems):
    def copy(block):
        rows = pl.ds(block * HALF, HALF)
        return pltpu.make_async_copy(out.at[rows], held.at[rows], sems.at[block])

    def put(block):
        rows = pl.ds(block * HALF, HALF)
        return pltpu.make_async_copy(held.at[rows], out.at[rows], out_sems.at[block])

    for block in range(4):
        copy(block).start()
    for slot in range(2):
        for half in range(2):
            block = slot * 2 + half
            copy(block).wait()
            rows = slice(block * HALF, (block + 1) * HALF)
            for h in range(2):
                columns = slice(h * HALF, (h + 1) * HALF)
                turned = mirror[:, h, slot, :, half * HALF : (half + 1) * HALF]
                held[rows, columns] = held[rows, columns] + turned.reshape(HALF, HALF).T
            put(block).start()
    for block in range(4):
        put(block).wait()


def join(direct, mirror):
    anywhere = pl.BlockSpec(memory_space=pl.ANY)
    return pl.pallas_call(
        join_kernel,
        out_shape=jax.ShapeDtypeStruct((2 * T, T), jnp.float32),
        in_specs=[anywhere, pl.BlockSpec(memory_space=pltpu.VMEM)],
        out_specs=anywhere,
        scratch_shapes=[
            pltpu.VMEM((2 * T, T), jnp.float32),
            pltpu.SemaphoreType.DMA((4,)),
            pltpu.SemaphoreType.DMA((4,)),
        ],
        input_output_aliases={0: 0},
        compiler_params=pltpu.CompilerParams(vmem_limit_bytes=24 << 20),
        cost_estimate=pl.CostEstimate(flops=1 << 20, bytes_accessed=6 << 20, transcendentals=0),
        name="join",
    )(direct, mirror)


def on_device(coeffs, hamiltonian_tiles, source_lists, present):
    xl, core, y, z = (lax.axis_index(a).astype(jnp.int32) for a in ("xl", "core", "y", "z"))
    matrices = hamiltonian_tiles[0]

    small = jnp.concatenate([source_lists[0], present.reshape(-1)]).astype(jnp.int32)
    both = [(i, 3 - i) for i in range(4)]
    four = jnp.stack(
        [
            small,
            lax.ppermute(small, "core", SWAP),
            lax.ppermute(small, "xl", SWAP),
            lax.ppermute(small, ("xl", "core"), both),
        ]
    )

    slots = coeffs.reshape(2, 2, HALF, T)

    def piece(slot, half):
        return lax.dynamic_slice(slots, (slot, half, 0, 0), (1, 1, HALF, T)).reshape(HALF, T)

    other_slot = lax.dynamic_slice(slots, (1 - core, 0, 0, 0), (1, 2, HALF, T))[0]
    from_core = lax.ppermute(other_slot, "core", SWAP)
    near = [piece(core, xl), lax.dynamic_slice(from_core, (xl, 0, 0), (1, HALF, T))[0]]
    send = [piece(core, 1 - xl), lax.dynamic_slice(from_core, (1 - xl, 0, 0), (1, HALF, T))[0]]
    local = near + [lax.ppermute(s, "xl", SWAP) for s in send]
    up = [lax.ppermute(t, "y", along_y(1)) for t in local]
    down = [lax.ppermute(t, "y", along_y(-1)) for t in local]
    onward = [lax.ppermute((up, down)[i % 2][i], "y", along_y((1, -1)[i % 2])) for i in range(4)]
    tiles = local + down + onward + up

    core_m = lax.ppermute(matrices, "core", SWAP)
    strips = matrices.reshape(4 * T, T)
    cut_z = lax.dynamic_slice(strips, (2 * T + z * HALF, 0), (HALF, T))
    cut_a, cut_b = matrices[0], matrices[1]
    far_a = lax.ppermute(cut_a, ("xh", "xl"), OUTER)
    far_b = lax.ppermute(cut_b, "xl", SWAP)
    near_z = lax.ppermute(cut_z, ("xh", "xl"), OUTER)
    far_z = [
        near_z,
        lax.ppermute(near_z, "z", along_y(-1)),
        lax.ppermute(near_z, "z", along_y(2)),
        lax.ppermute(near_z, "z", along_y(1)),
    ]
    far = [far_a, far_b] + far_z
    farther = [lax.ppermute(cut, "core", SWAP) for cut in far]

    def quarter(q, pieces):
        return [(p, (0, HALF), (q, step, step == 3)) for step, p in enumerate(pieces)]

    matrix = [[[(m, slot)] for slot in range(4)] for m in (matrices, core_m)]
    matrix += [
        [[(f[0], (0, T))], [(f[1], (0, T))]]
        + [quarter(2 * s, f[2:]) + quarter(2 * s + 1, f[2:]) for s in range(2)]
        for f in (far, farther)
    ]

    column = y * 4 + xl * 2 + core
    own = jnp.stack([column, column ^ 1, column ^ 2, column ^ 3])
    sources = jnp.concatenate([own[:, None], four[:, :3]], axis=1)
    place = ((sources // 4 - y) % 4) * 4 + ((sources ^ column) & 3)
    where = jnp.stack([xl, core, z])
    table = jnp.concatenate([place.reshape(-1), where, four[:, 3:].reshape(-1)])

    unit = 6 * HALF * T * T

    def pick(ids):
        return [tiles[i] for i in ids]

    def in_middle(j, m, t):
        return jnp.where(j < 2, one_of(t, MIDDLE), jnp.logical_not(one_of(t, LATE + LAST)))

    four_columns = (0, 1, 2, 3)
    sums = products(
        table, pick(EARLY), matrix[:2], [], (0, 1), EARLY,
        lambda j, m, t: one_of(t, EARLY), [SUM] * 2, False, 5 * unit,
    )
    sums = products(
        table, pick(EARLY + MIDDLE), matrix, sums, four_columns, EARLY + MIDDLE,
        in_middle, [SUM] * 4 + [MIRROR], False, 8 * unit,
    )
    for ids in (LATE, LAST):
        sums = products(
            table, pick(ids), matrix, sums, four_columns, ids,
            lambda j, m, t, ids=ids: one_of(t, ids), [SUM] * 4 + [MIRROR], True, 2 * unit,
        )
    mirror = sums[4]
    near, core_near, far_near, far_core = (m.reshape(HALF, T) for m in sums[:4])
    d01 = lax.ppermute(far_near, "xl", SWAP)
    from_far = lax.ppermute(far_core, "xl", SWAP)
    d10 = lax.ppermute(core_near, "core", SWAP)
    d11 = lax.ppermute(from_far, "core", SWAP)

    spread = lax.all_to_all(
        mirror.reshape(32, 32, T), ("xh", "z", "y"), split_axis=0, concat_axis=0, tiled=True
    )
    spread = spread.reshape(2, 2, 2, 2, 2, 2, 16, T).transpose(3, 4, 5, 0, 1, 2, 6, 7)
    owned = lax.all_to_all(
        spread.reshape(64, 16, T), ("xh", "z", "y", "xl"), split_axis=0, concat_axis=0, tiled=True
    )
    direct = assemble(where, near, d01, d10, d11)
    return join(direct, owned.reshape(32, 2, 2, 8, T))


def solution(mesh):
    fine = Mesh(mesh.devices.reshape(SIZES), AXES)
    row, col = ("xh", "z"), ("y", "xl", "core")
    placed = (P(row, col), P(col, None, None, None), P(col, None), P(col, None, None, None))

    return jax.shard_map(on_device, mesh=fine, in_specs=placed, out_specs=P(row, col), check_vma=False)
```
